32 devices in a mesh: path: 4 (over z), trade: 8 (over y, x, core).
Axes of the slice: x: 2, y: 2, z: 4, core: 2. Of those that a mesh axis runs over, the one named last changes fastest.
Arguments:
- factors: bfloat16 [32, 8, 512], P(None, None, 'path'), may hold values from -5 to 5
- loadings: bfloat16 [32, 8, 32768], P(None, None, 'trade'), may hold values from -0.5 to 0.5
- notional: float32 [32768], P('trade'), may hold values from -1 to 1
- strike: float32 [32768], P('trade'), may hold values from 0.5 to 1.5
- date_weight: float32 [32], replicated, may hold values from 0.3 to 3
- loss_spanning: float32 [128], replicated, may hold values from 0.2 to 0.9
- loss_local: float32 [1024], P('trade'), may hold values from 0.2 to 0.9
- trade_slot: int32 [32768], P('trade'), may hold values from 0 to 255
- span_list: int32 [1024], P('trade'), may hold values from 0 to 127, as said below
Outputs:
- loading_grad: float32 [32, 8, 32768], P('path', None, 'trade')
- factor_grad: float32 [32, 8, 512], P('trade', None, 'path')
The draws below stay inside these ranges and needn't reach their ends.
Inputs may be any that keep to these rules, and one draw needn't show every extreme that they name: `trade_slot`: slot s < 128 of a trade shard holds that shard's spanning set from span_list; slot 128 + i holds the shard's i-th local set. `span_list`: the 128 entries of one trade shard are distinct spanning set ids.
All inputs are finite; a program needn't handle non-finite values.
Results may differ from the reference program's by a relative error of at most 0.0021.
Values may be sent and summed in bfloat16 or wider, within the bound.
A program may use at most 64 MiB of HBM per device.

```python
import math
import jax
import jax.numpy as jnp
import numpy as np
from jax import lax

FACTORS = 8
DATES = 32
K_DEV = 4096
SLOTS = 256
SPAN_DEV = 128
LOC_DEV = 128
SPAN_ALL = 128
TRADES = 32768
PATHS = 512
N_TRADE = 8


def draw_span_list(key, part):
    shard_keys = jax.random.split(jax.random.fold_in(key, 11), N_TRADE)
    shards = jnp.arange(N_TRADE, dtype=jnp.int32)

    def one_shard(shard_key, shard):
        order = jax.random.permutation(shard_key, SPAN_ALL).astype(jnp.int32)
        wanted = (shard * (SPAN_ALL - 1) // max(N_TRADE - 1, 1)).astype(jnp.int32)
        position = jnp.argmax(order == wanted)
        leading = order[0]
        order = order.at[position].set(leading).at[0].set(wanted)
        return order[:SPAN_DEV]
    return jax.vmap(one_shard)(shard_keys, shards).reshape(N_TRADE * SPAN_DEV)


def with_ends(result, rng, least, high):
    extent = result.shape
    spot = [jax.random.randint(jax.random.fold_in(rng, axis), (), 0, extent[axis]) for axis in range(len(extent))]
    result = result.at[tuple(spot)].set(least)
    longest = extent.index(max(extent))
    spot[longest] = (spot[longest] + 1) % extent[longest]
    return result.at[tuple(spot)].set(high)


def steps_of(key, extent, cuts, smallest, largest):
    level, own = 1.0, jax.random.fold_in(key, 6)
    for dim, blocks in cuts:
        draws = jnp.exp(jax.random.uniform(jax.random.fold_in(own, dim), (blocks,), jnp.float32, smallest / len(cuts), largest / len(cuts)))
        level = level * jnp.repeat(draws, extent[dim] // blocks).reshape([-1 if axis == dim else 1 for axis in range(len(extent))])
    return level


def rank_table(count, skew):
    portions = [(1 << 20) // math.isqrt(rank ** skew) + 1 for rank in range(1, count + 1)]
    deviation = 1 + sum(portions) // (1 << 30)
    return np.cumsum(np.array([max(1, weight // deviation) for weight in portions]))


def ranked(key, dims, amount, skew):
    grid = rank_table(amount, skew)
    ticket = jax.random.randint(jax.random.fold_in(key, 1), dims, 0, int(grid[amount - 1]))
    grade = jnp.searchsorted(jnp.asarray(grid, jnp.int32), ticket, side="right")
    return jax.random.permutation(jax.random.fold_in(key, 2), amount)[grade].astype(jnp.int32)


def normal_values(key, dims, spread, limit, cuts=(), held_as=jnp.bfloat16):
    gain = steps_of(key, dims, cuts, -0.22, 0.18) if cuts else 1.0
    drawn = jax.random.normal(key, dims, jnp.float32) * spread * gain
    return jnp.minimum(jnp.maximum(drawn, -limit), limit).astype(held_as)


def setup_inputs(seed: int = 0) -> dict:
    key_list = jax.random.split(jax.random.key(seed), 10)
    return {
        "factors": normal_values(key_list[0], (DATES, FACTORS, PATHS), 1.0, 5.0, ((2, 4),)),
        "loadings": normal_values(key_list[1], (DATES, FACTORS, TRADES), 0.12, 0.5, ((2, 8),)),
        "notional": jnp.clip(jax.random.uniform(key_list[2], (TRADES,), jnp.float32, -1.0, 1.0) * steps_of(key_list[2], (TRADES,), ((0, 8),), -0.4, 0.0), -1.0, 1.0),
        "strike": jnp.clip(0.5 + 1.0 * jax.random.uniform(key_list[3], (TRADES,), jnp.float32) ** steps_of(key_list[3], (TRADES,), ((0, 8),), -0.2, 0.2), 0.5, 1.5),
        "date_weight": jnp.clip(jnp.exp(jax.random.uniform(key_list[4], (DATES,), jnp.float32, math.log(0.3), math.log(3.0))), 0.3, 3.0),
        "loss_spanning": jnp.clip(jax.random.uniform(key_list[5], (SPAN_ALL,), jnp.float32, 0.2, 0.9), 0.2, 0.9),
        "loss_local": jnp.clip(0.2 + 0.7 * jax.random.uniform(key_list[6], (N_TRADE * LOC_DEV,), jnp.float32) ** steps_of(key_list[6], (N_TRADE * LOC_DEV,), ((0, 8),), -0.2, 0.2), 0.2, 0.9),
        "trade_slot": with_ends(ranked(key_list[7], (TRADES,), SLOTS, 2), jax.random.fold_in(key_list[7], 3), 0, SLOTS - 1).astype(jnp.int32),
        "span_list": draw_span_list(jax.random.fold_in(key_list[9], 71), 0),
    }


smoothing = 0.5


def reference(factors, loadings, notional, strike, date_weight, loss_spanning, loss_local, trade_slot, span_list):
    shard_of = (jnp.arange(TRADES) // K_DEV).astype(jnp.int32)
    global_slot = (shard_of * SLOTS + trade_slot).astype(jnp.int32)
    path_count = factors.shape[2]

    def one_date(date_index):
        factor_now = factors[date_index]
        loading_now = loadings[date_index]
        exponent = jnp.dot(factor_now.T, loading_now, preferred_element_type=jnp.float32)
        growth = jnp.exp(exponent)
        values = (notional[None, :] * (growth - strike[None, :])).astype(jnp.bfloat16)
        partial_sums = jax.ops.segment_sum(values.astype(jnp.float32).T, global_slot, N_TRADE * SLOTS).T
        partial_sums = partial_sums.reshape(path_count, N_TRADE, SLOTS)
        span_part = partial_sums[:, :, :SPAN_DEV].reshape(path_count, N_TRADE * SPAN_DEV)
        span_total = jax.ops.segment_sum(span_part.T, span_list, SPAN_ALL).T
        weight_now = date_weight[date_index]
        span_weight = (weight_now * loss_spanning[None, :] * jax.nn.sigmoid(span_total / smoothing)).astype(jnp.bfloat16)
        local_total = partial_sums[:, :, SPAN_DEV:].reshape(path_count, N_TRADE * LOC_DEV)
        local_weight = (weight_now * loss_local[None, :] * jax.nn.sigmoid(local_total / smoothing)).astype(jnp.bfloat16)
        span_slots = span_weight[:, span_list].reshape(path_count, N_TRADE, SPAN_DEV)
        slot_weight = jnp.concatenate([span_slots, local_weight.reshape(path_count, N_TRADE, LOC_DEV)], axis=2)
        slot_weight = slot_weight.reshape(path_count, N_TRADE * SLOTS)
        trade_weight = slot_weight[:, global_slot].astype(jnp.float32)
        sensitivity = (trade_weight * notional[None, :] * growth).astype(jnp.bfloat16)
        loading_grad = jnp.dot(factor_now, sensitivity, preferred_element_type=jnp.float32) / path_count
        factor_grad = jnp.dot(loading_now, sensitivity.T, preferred_element_type=jnp.float32)
        return loading_grad, factor_grad

    loading_grads, factor_grads = lax.map(one_date, jnp.arange(DATES).astype(jnp.int32))
    return loading_grads, factor_grads
```

```python
import functools
import math

import jax
import jax.numpy as jnp
from jax import lax
from jax.experimental import pallas as pl
from jax.experimental.pallas import tpu as pltpu
from jax.sharding import PartitionSpec as P

smoothing = 0.5
MESH = pl.DeviceIdType.MESH
bf16 = jnp.bfloat16
f32 = jnp.float32
f8 = jnp.float8_e4m3fn


def chunk_of(paths, trades):
    return math.gcd(trades, (1 << 20) // paths)


def dot(a, b):
    return jnp.dot(a, b, preferred_element_type=f32)


factor_pieces = 4
loading_pieces = 2
factor_scale = 2.0**5
loading_scale = 2.0**9


def pieces_of(x, count):
    pieces = []
    for _ in range(count):
        piece = x.astype(f8).astype(f32)
        pieces.append(piece)
        x = x - piece
    return pieces


def kernel(
    n_path,
    n_trade,
    factors_hbm,
    loadings_hbm,
    notional_hbm,
    strike_hbm,
    date_weight_hbm,
    loss_span_hbm,
    loss_local_hbm,
    slot_hbm,
    span_hbm,
    loading_grad_ref,
    factor_grad_ref,
    growth,
    table,
    table_t,
    load_own,
    load_split,
    notional_ref,
    strike_ref,
    offset,
    date_weight_ref,
    loss_span_ref,
    loss_local_ref,
    slot_ref,
    span_ref,
    fac_recv,
    fac,
    fac_split,
    total,
    part,
    pair_recv,
    chip_sum,
    cross_recv,
    local_w,
    span_half,
    span_other,
    slot_w,
    factor_acc,
    grad_send,
    grad_recv,
    ready_sem,
    in_sem,
    fac_ssem,
    fac_rsem,
    pair_ssem,
    pair_rsem,
    cross_ssem,
    cross_rsem,
    half_ssem,
    half_rsem,
    other_ssem,
    other_rsem,
    grad_ssem,
    grad_rsem,
):
    me_path = lax.axis_index("path")
    me_trade = lax.axis_index("trade")
    dates, factor_count, path_local = factors_hbm.shape
    dates_own = dates // n_path
    dates_out = dates // n_trade
    groups = dates_own // dates_out
    trades = loadings_hbm.shape[2]
    spans = loss_span_ref.shape[1]
    span_slots = span_ref.shape[1]
    locals_ = loss_local_ref.shape[1]
    slots = span_slots + locals_
    path_total = n_path * path_local
    chunk = chunk_of(path_total, trades)
    steps = trades // chunk
    first_date = me_path * dates_own
    rows = path_total // n_trade
    chips = n_trade // 2
    me_chip = me_trade // 2
    me_core = lax.rem(me_trade, 2)
    sibling = me_trade + 1 - 2 * me_core

    def path_at(step):
        return lax.rem(me_path + step + n_path, n_path)

    def trade_at(step):
        return lax.rem(me_trade + step + n_trade, n_trade)

    def chip_at(step):
        return lax.rem(me_chip + step + chips, chips)

    def columns(c):
        return pl.ds(pl.multiple_of(c * chunk, chunk), chunk)

    def wait_all(buffer, sem):
        pltpu.make_async_copy(buffer, buffer, sem).wait()

    barrier = pltpu.get_barrier_semaphore()
    for a in range(1, n_path):
        pl.semaphore_signal(
            barrier, inc=1, device_id={"path": path_at(a)}, device_id_type=MESH
        )
    for b in range(1, n_trade):
        pl.semaphore_signal(
            barrier, inc=1, device_id={"trade": trade_at(b)}, device_id_type=MESH
        )

    own_dates = pl.ds(first_date, dates_own)
    inputs = [
        pltpu.make_async_copy(source, target, in_sem.at[i])
        for i, (source, target) in enumerate(
            (
                (slot_hbm, slot_ref),
                (span_hbm, span_ref),
                (loadings_hbm.at[own_dates], load_own),
                (factors_hbm.at[own_dates], fac_recv.at[0]),
                (notional_hbm, notional_ref),
                (strike_hbm, strike_ref),
                (date_weight_hbm, date_weight_ref),
                (loss_span_hbm, loss_span_ref),
                (loss_local_hbm, loss_local_ref),
            )
        )
    ]
    for copy in inputs:
        copy.start()
    for copy in inputs[:2]:
        copy.wait()

    set_match = (
        lax.broadcasted_iota(jnp.int32, (spans, span_slots), 0) == span_ref[...]
    ).astype(f32).astype(bf16)

    @pl.loop(0, steps)
    def _(c):
        cols = columns(c)
        hot = (
            lax.broadcasted_iota(jnp.int32, (slots, chunk), 0) == slot_ref[:, cols]
        ).astype(f32)
        span_hot = dot(set_match, hot[:span_slots].astype(bf16))
        both = jnp.concatenate([span_hot, hot[span_slots:]], axis=0)
        table_t[:, cols] = both.astype(bf16)
        table[cols, :] = both.T.astype(bf16)

    for copy in inputs[2:]:
        copy.wait()

    pl.semaphore_wait(barrier, n_path + n_trade - 2)

    def fac_copy(o):
        there = path_at(o)
        return pltpu.make_async_remote_copy(
            src_ref=factors_hbm.at[pl.ds(there * dates_own, dates_own)],
            dst_ref=fac_recv.at[o],
            send_sem=fac_ssem,
            recv_sem=fac_rsem,
            device_id={"path": there},
            device_id_type=MESH,
        )

    for o in range(1, n_path):
        fac_copy(o).start()
    for o in range(1, n_path):
        pl.semaphore_signal(
            ready_sem, inc=1, device_id={"path": path_at(o)}, device_id_type=MESH
        )

    offset[...] = notional_ref[...] * strike_ref[...]

    @pl.loop(0, dates_own)
    def _(d):
        pieces = pieces_of(load_own[d].astype(f32) * loading_scale, loading_pieces)
        load_split[d] = jnp.concatenate(pieces * factor_pieces, axis=0).astype(f8)

    def split_factors(first, last):
        @pl.loop(0, dates_own)
        def _(d):
            for o in range(first, last):
                block = fac_recv[o, d]
                at = pl.ds(o * path_local, path_local)
                fac[d, :, at] = block
                scaled = block.astype(f32) * f32(math.log2(math.e)) * factor_scale
                split = [
                    piece
                    for piece in pieces_of(scaled, factor_pieces)
                    for _ in range(loading_pieces)
                ]
                fac_split[d, at, :] = jnp.concatenate(split, axis=0).T.astype(f8)

    def phase_one(d, first, last):
        at = slice(first, last)
        total[at, :] = jnp.zeros((last - first, total.shape[1]), f32)

        @pl.loop(0, steps, unroll=True)
        def _(c):
            cols = columns(c)
            exponent = dot(fac_split[d, at, :], load_split[d, :, cols])
            exponent = exponent * (1.0 / (factor_scale * loading_scale))
            grown = jnp.exp2(exponent) * notional_ref[:, cols]
            growth[d * steps + c, at, :] = grown.astype(bf16)
            values = (grown - offset[:, cols]).astype(bf16)
            total[at, :] += dot(values, table[cols, :])

        for r in range(first // rows, last // rows):
            part[d, r % 2, r // 2] = total[r * rows : (r + 1) * rows, :spans]
        weight = date_weight_ref[first_date + d]
        local_w[d, at, :] = (
            weight
            * loss_local_ref[...]
            * jax.nn.sigmoid(total[at, spans:] / smoothing)
        ).astype(bf16)

    split_factors(0, 1)

    @pl.loop(0, dates_own)
    def _(d):
        phase_one(d, 0, path_local)

    if n_path > 1:
        wait_all(fac_recv.at[pl.ds(1, n_path - 1)], fac_rsem)
        split_factors(1, n_path)

    def send_pair(d):
        pltpu.make_async_remote_copy(
            src_ref=part.at[d, 1 - me_core],
            dst_ref=pair_recv.at[d],
            send_sem=pair_ssem.at[d],
            recv_sem=pair_rsem.at[d],
            device_id={"trade": sibling},
            device_id_type=MESH,
        ).start()

    def send_cross(d):
        wait_all(pair_recv.at[d], pair_rsem.at[d])
        chip_sum[d] = part[d, me_core] + pair_recv[d]
        for o in range(1, chips):
            there = chip_at(o)
            pltpu.make_async_remote_copy(
                src_ref=chip_sum.at[d, there],
                dst_ref=cross_recv.at[d, o - 1],
                send_sem=cross_ssem.at[d],
                recv_sem=cross_rsem.at[d],
                device_id={"trade": there * 2 + me_core},
                device_id_type=MESH,
            ).start()

    def send_half(d):
        wait_all(cross_recv.at[d], cross_rsem.at[d])
        sums = chip_sum[d, me_chip]
        for o in range(1, chips):
            sums = sums + cross_recv[d, o - 1]
        weight = date_weight_ref[first_date + d]
        span_half[d, 0] = (
            weight * loss_span_ref[...] * jax.nn.sigmoid(sums / smoothing)
        ).astype(bf16)
        for o in range(1, chips):
            pltpu.make_async_remote_copy(
                src_ref=span_half.at[d, 0],
                dst_ref=span_half.at[d, o],
                send_sem=half_ssem.at[d],
                recv_sem=half_rsem.at[d],
                device_id={"trade": chip_at(o) * 2 + me_core},
                device_id_type=MESH,
            ).start()

    def send_other(d):
        wait_all(span_half.at[d, pl.ds(1, chips - 1)], half_rsem.at[d])
        pltpu.make_async_remote_copy(
            src_ref=span_half.at[d],
            dst_ref=span_other.at[d],
            send_sem=other_ssem.at[d],
            recv_sem=other_rsem.at[d],
            device_id={"trade": sibling},
            device_id_type=MESH,
        ).start()

    lag = max(1, (dates_own - 1) // 3)
    stages = ((lag, send_cross), (2 * lag, send_half), (3 * lag, send_other))

    @pl.loop(0, dates_own)
    def _(d):
        if n_path > 1:
            phase_one(d, path_local, path_total)
        send_pair(d)

        for late, stage in stages:

            @pl.when(d >= late)
            def _(late=late, stage=stage):
                stage(d - late)

    def grad_copy(g, o):
        return pltpu.make_async_remote_copy(
            src_ref=grad_send.at[g, o],
            dst_ref=grad_recv.at[me_trade],
            send_sem=grad_ssem.at[g, o],
            recv_sem=grad_rsem.at[me_trade],
            device_id={"path": path_at(-o), "trade": me_path * groups + g},
            device_id_type=MESH,
        )

    if n_path > 1:
        pl.semaphore_wait(ready_sem, n_path - 1)

    @pl.loop(0, dates_own)
    def _(d):
        wait_all(span_other.at[d], other_rsem.at[d])
        for o in range(chips):
            for core, source in ((me_core, span_half), (1 - me_core, span_other)):
                start = pl.multiple_of((chip_at(-o) * 2 + core) * rows, rows)
                slot_w[pl.ds(start, rows), :spans] = source[d, o]
        slot_w[:, spans:] = local_w[d]

        @pl.loop(0, steps, unroll=True)
        def _(c):
            weight = dot(slot_w[...], table_t[:, columns(c)]).astype(bf16)
            growth[d * steps + c] = weight * growth[d * steps + c]

        factor_acc[...] = jnp.zeros_like(factor_acc)

        @pl.loop(0, steps, unroll=True)
        def _(c):
            factor_acc[...] += lax.dot_general(
                load_own[d, :, columns(c)],
                growth[d * steps + c],
                (((1,), (1,)), ((), ())),
                preferred_element_type=f32,
            )

        g = d // dates_out
        for o in range(n_path):
            grad_send[g, o, lax.rem(d, dates_out)] = factor_acc[
                :, o * path_local : (o + 1) * path_local
            ]

        for late, stage in stages:

            @pl.when(d < late)
            def _(late=late, stage=stage):
                stage(d + dates_own - late)

        @pl.when(lax.rem(d, dates_out) == dates_out - 1)
        def _():
            here = me_path * groups + g == me_trade

            @pl.when(here)
            def _():
                pltpu.make_async_copy(
                    grad_send.at[g, 0], grad_recv.at[me_trade], grad_rsem.at[me_trade]
                ).start()

            @pl.when(jnp.logical_not(here))
            def _():
                grad_copy(g, 0).start()

            for o in range(1, n_path):
                grad_copy(g, o).start()

    @pl.loop(0, dates_own)
    def _(d):
        @pl.loop(0, steps, unroll=True)
        def _(c):
            loading_grad_ref[d, :, columns(c)] = (
                dot(fac[d], growth[d * steps + c]) / path_total
            )

    if n_path > 1:
        wait_all(fac_recv.at[pl.ds(1, n_path - 1)], fac_ssem)
    for d in range(dates_own):
        wait_all(pair_recv.at[d], pair_ssem.at[d])
        wait_all(cross_recv.at[d], cross_ssem.at[d])
        wait_all(span_half.at[d, pl.ds(1, chips - 1)], half_ssem.at[d])
        wait_all(span_other.at[d], other_ssem.at[d])
    for g in range(groups):

        @pl.when(me_path * groups + g != me_trade)
        def _():
            grad_copy(g, 0).wait_send()

        for o in range(1, n_path):
            grad_copy(g, o).wait_send()

    for b in range(n_trade):
        wait_all(grad_recv.at[b], grad_rsem.at[b])
    sums = grad_recv[0]
    for b in range(1, n_trade):
        sums = sums + grad_recv[b]
    factor_grad_ref[...] = sums


def on_device(
    n_path,
    n_trade,
    factors,
    loadings,
    notional,
    strike,
    date_weight,
    loss_spanning,
    loss_local,
    trade_slot,
    span_list,
):
    dates, factor_count, path_local = factors.shape
    trades = loadings.shape[2]
    spans = loss_spanning.shape[0]
    locals_ = loss_local.shape[0]
    span_slots = span_list.shape[0]
    width = spans + locals_
    paths = n_path * path_local
    rows = paths // n_trade
    chips = n_trade // 2
    dates_own = dates // n_path
    dates_out = dates // n_trade
    groups = dates_own // dates_out
    chunk = chunk_of(paths, trades)
    depth = factor_pieces * loading_pieces * factor_count
    vmem = pl.BlockSpec(memory_space=pltpu.VMEM)
    dma = pltpu.SemaphoreType.DMA
    return pl.pallas_call(
        functools.partial(kernel, n_path, n_trade),
        out_shape=(
            pltpu.VMEM((dates_own, factor_count, trades), f32),
            pltpu.VMEM((dates_out, factor_count, path_local), f32),
        ),
        in_specs=[pl.BlockSpec(memory_space=pl.ANY)] * 9,
        out_specs=(vmem, vmem),
        scratch_shapes=[
            pltpu.VMEM((dates_own * (trades // chunk), paths, chunk), bf16),
            pltpu.VMEM((trades, width), bf16),
            pltpu.VMEM((width, trades), bf16),
            pltpu.VMEM((dates_own, factor_count, trades), bf16),
            pltpu.VMEM((dates_own, depth, trades), f8),
            pltpu.VMEM((1, trades), f32),
            pltpu.VMEM((1, trades), f32),
            pltpu.VMEM((1, trades), f32),
            pltpu.SMEM((dates,), f32),
            pltpu.VMEM((1, spans), f32),
            pltpu.VMEM((1, locals_), f32),
            pltpu.VMEM((1, trades), jnp.int32),
            pltpu.VMEM((1, span_slots), jnp.int32),
            pltpu.VMEM((n_path, dates_own, factor_count, path_local), bf16),
            pltpu.VMEM((dates_own, factor_count, paths), bf16),
            pltpu.VMEM((dates_own, paths, depth), f8),
            pltpu.VMEM((paths, width), f32),
            pltpu.VMEM((dates_own, 2, chips, rows, spans), f32),
            pltpu.VMEM((dates_own, chips, rows, spans), f32),
            pltpu.VMEM((dates_own, chips, rows, spans), f32),
            pltpu.VMEM((dates_own, chips - 1, rows, spans), f32),
            pltpu.VMEM((dates_own, paths, locals_), bf16),
            pltpu.VMEM((dates_own, chips, rows, spans), bf16),
            pltpu.VMEM((dates_own, chips, rows, spans), bf16),
            pltpu.VMEM((paths, width), bf16),
            pltpu.VMEM((factor_count, paths), f32),
            pltpu.VMEM((groups, n_path, dates_out, factor_count, path_local), f32),
            pltpu.VMEM((n_trade, dates_out, factor_count, path_local), f32),
            pltpu.SemaphoreType.REGULAR,
            dma((9,)),
            dma,
            dma,
            dma((dates_own,)),
            dma((dates_own,)),
            dma((dates_own,)),
            dma((dates_own,)),
            dma((dates_own,)),
            dma((dates_own,)),
            dma((dates_own,)),
            dma((dates_own,)),
            dma((groups, n_path)),
            dma((n_trade,)),
        ],
        compiler_params=pltpu.CompilerParams(
            collective_id=0, has_side_effects=True, vmem_limit_bytes=61 << 20
        ),
    )(
        factors,
        loadings,
        notional[None],
        strike[None],
        date_weight,
        loss_spanning[None],
        loss_local[None],
        trade_slot[None],
        span_list[None],
    )


def solution(mesh):
    return jax.shard_map(
        functools.partial(on_device, mesh.shape["path"], mesh.shape["trade"]),
        mesh=mesh,
        in_specs=(
            P(None, None, "path"),
            P(None, None, "trade"),
            P("trade"),
            P("trade"),
            P(),
            P(),
            P("trade"),
            P("trade"),
            P("trade"),
        ),
        out_specs=(P("path", None, "trade"), P("trade", None, "path")),
        check_vma=False,
    )
```

```python
import functools
import math

import jax
import jax.numpy as jnp
from jax import lax
from jax.experimental import pallas as pl
from jax.experimental.pallas import tpu as pltpu
from jax.sharding import PartitionSpec as P

smoothing = 0.5
vmem_bytes = 254 << 18
MESH = pl.DeviceIdType.MESH
bf16 = jnp.bfloat16
f32 = jnp.float32


def chunk_of(paths, trades):
    return math.gcd(trades, (1 << 21) // paths)


def dot(a, b):
    return jnp.dot(a, b, preferred_element_type=f32)


def kernel(
    n_path,
    n_trade,
    factors_hbm,
    loadings_hbm,
    notional_hbm,
    strike_hbm,
    date_weight_hbm,
    loss_span_hbm,
    loss_local_hbm,
    slot_hbm,
    span_hbm,
    loading_grad_ref,
    factor_grad_ref,
    growth,
    table,
    table_t,
    load_own,
    load_split,
    notional_ref,
    strike_ref,
    offset,
    date_weight_ref,
    loss_span_ref,
    loss_local_ref,
    slot_ref,
    span_ref,
    fac_recv,
    fac,
    fac_split,
    part,
    pair_recv,
    chip_sum,
    cross_recv,
    local_w,
    span_half,
    span_other,
    slot_w,
    grad_send,
    grad_recv,
    ready_sem,
    in_sem,
    fac_ssem,
    fac_rsem,
    pair_ssem,
    pair_rsem,
    cross_ssem,
    cross_rsem,
    half_ssem,
    half_rsem,
    other_ssem,
    other_rsem,
    grad_ssem,
    grad_rsem,
):
    me_path = lax.axis_index("path")
    me_trade = lax.axis_index("trade")
    dates, factor_count, path_local = factors_hbm.shape
    dates_own = dates // n_path
    dates_out = dates // n_trade
    groups = dates_own // dates_out
    trades = loadings_hbm.shape[2]
    spans = loss_span_ref.shape[1]
    span_slots = span_ref.shape[1]
    locals_ = loss_local_ref.shape[1]
    slots = span_slots + locals_
    path_total = n_path * path_local
    chunk = chunk_of(path_total, trades)
    steps = trades // chunk
    first_date = me_path * dates_own
    rows = path_total // n_trade
    chips = n_trade // 2
    me_chip = me_trade // 2
    me_core = lax.rem(me_trade, 2)
    sibling = me_trade + 1 - 2 * me_core

    def path_at(step):
        return lax.rem(me_path + step + n_path, n_path)

    def trade_at(step):
        return lax.rem(me_trade + step + n_trade, n_trade)

    def chip_at(step):
        return lax.rem(me_chip + step + chips, chips)

    def columns(c):
        return pl.ds(pl.multiple_of(c * chunk, chunk), chunk)

    def wait_all(buffer, sem):
        pltpu.make_async_copy(buffer, buffer, sem).wait()

    barrier = pltpu.get_barrier_semaphore()
    for a in range(1, n_path):
        pl.semaphore_signal(
            barrier, inc=1, device_id={"path": path_at(a)}, device_id_type=MESH
        )
    for b in range(1, n_trade):
        pl.semaphore_signal(
            barrier, inc=1, device_id={"trade": trade_at(b)}, device_id_type=MESH
        )

    own_dates = pl.ds(first_date, dates_own)
    inputs = [
        pltpu.make_async_copy(source, target, in_sem.at[i])
        for i, (source, target) in enumerate(
            (
                (slot_hbm, slot_ref),
                (span_hbm, span_ref),
                (loadings_hbm.at[own_dates], load_own),
                (factors_hbm.at[own_dates], fac_recv.at[0]),
                (notional_hbm, notional_ref),
                (strike_hbm, strike_ref),
                (date_weight_hbm, date_weight_ref),
                (loss_span_hbm, loss_span_ref),
                (loss_local_hbm, loss_local_ref),
            )
        )
    ]
    for copy in inputs:
        copy.start()
    for copy in inputs[:2]:
        copy.wait()

    set_match = (
        lax.broadcasted_iota(jnp.int32, (spans, span_slots), 0) == span_ref[...]
    ).astype(f32).astype(bf16)

    @pl.loop(0, steps)
    def _(c):
        cols = columns(c)
        hot = (
            lax.broadcasted_iota(jnp.int32, (slots, chunk), 0) == slot_ref[:, cols]
        ).astype(f32)
        span_hot = dot(set_match, hot[:span_slots].astype(bf16))
        both = jnp.concatenate([span_hot, hot[span_slots:]], axis=0)
        table_t[:, cols] = both.astype(bf16)
        table[cols, :] = both.T.astype(bf16)

    for copy in inputs[2:]:
        copy.wait()

    pl.semaphore_wait(barrier, n_path + n_trade - 2)

    def fac_copy(o):
        there = path_at(o)
        return pltpu.make_async_remote_copy(
            src_ref=factors_hbm.at[pl.ds(there * dates_own, dates_own)],
            dst_ref=fac_recv.at[o],
            send_sem=fac_ssem,
            recv_sem=fac_rsem,
            device_id={"path": there},
            device_id_type=MESH,
        )

    for o in range(1, n_path):
        fac_copy(o).start()
    for o in range(1, n_path):
        pl.semaphore_signal(
            ready_sem, inc=1, device_id={"path": path_at(o)}, device_id_type=MESH
        )

    offset[...] = notional_ref[...] * strike_ref[...]

    @pl.loop(0, dates_own)
    def _(d):
        row = load_own[d]
        load_split[d] = jnp.concatenate([row, row, row, row], axis=0)

    def split_factors(first, last):
        @pl.loop(0, dates_own)
        def _(d):
            for o in range(first, last):
                block = fac_recv[o, d]
                at = pl.ds(o * path_local, path_local)
                fac[d, :, at] = block
                scaled = block.astype(f32) * f32(math.log2(math.e))
                high = scaled.astype(bf16).astype(f32)
                middle = (scaled - high).astype(bf16).astype(f32)
                low = scaled - high - middle
                split = [high, middle, low, jnp.zeros_like(low)]
                fac_split[d, at, :] = jnp.concatenate(split, axis=0).T.astype(bf16)

    def phase_one(d, first, last):
        at = slice(first, last)
        total = None
        for c in range(steps):
            cols = slice(c * chunk, (c + 1) * chunk)
            exponent = dot(fac_split[d, at, :], load_split[d, :, cols])
            grown = jnp.exp2(exponent) * notional_ref[:, cols]
            growth[d * steps + c, at, :] = grown.astype(bf16)
            values = (grown - offset[:, cols]).astype(bf16)
            sums = dot(values, table[cols, :])
            total = sums if total is None else total + sums

        for r in range(first // rows, last // rows):
            here = slice(r * rows - first, (r + 1) * rows - first)
            part[d, r % 2, r // 2] = total[here, :spans]
        weight = date_weight_ref[first_date + d]
        local_w[d, at, :] = (
            weight
            * loss_local_ref[...]
            * jax.nn.sigmoid(total[:, spans:] / smoothing)
        ).astype(bf16)

    split_factors(0, 1)
    unroll = math.gcd(dates_own, 4)

    @pl.loop(0, dates_own // unroll)
    def _(block):
        for i in range(unroll):
            phase_one(block * unroll + i, 0, path_local)

    if n_path > 1:
        wait_all(fac_recv.at[pl.ds(1, n_path - 1)], fac_rsem)
        split_factors(1, n_path)

    def send_pair(d):
        pltpu.make_async_remote_copy(
            src_ref=part.at[d, 1 - me_core],
            dst_ref=pair_recv.at[d],
            send_sem=pair_ssem.at[d],
            recv_sem=pair_rsem.at[d],
            device_id={"trade": sibling},
            device_id_type=MESH,
        ).start()

    def send_cross(d):
        wait_all(pair_recv.at[d], pair_rsem.at[d])
        chip_sum[d] = part[d, me_core] + pair_recv[d]
        for o in range(1, chips):
            there = chip_at(o)
            pltpu.make_async_remote_copy(
                src_ref=chip_sum.at[d, there],
                dst_ref=cross_recv.at[d, o - 1],
                send_sem=cross_ssem.at[d],
                recv_sem=cross_rsem.at[d],
                device_id={"trade": there * 2 + me_core},
                device_id_type=MESH,
            ).start()

    def send_half(d):
        wait_all(cross_recv.at[d], cross_rsem.at[d])
        sums = chip_sum[d, me_chip]
        for o in range(1, chips):
            sums = sums + cross_recv[d, o - 1]
        weight = date_weight_ref[first_date + d]
        span_half[d, 0] = (
            weight * loss_span_ref[...] * jax.nn.sigmoid(sums / smoothing)
        ).astype(bf16)
        for o in range(1, chips):
            pltpu.make_async_remote_copy(
                src_ref=span_half.at[d, 0],
                dst_ref=span_half.at[d, o],
                send_sem=half_ssem.at[d],
                recv_sem=half_rsem.at[d],
                device_id={"trade": chip_at(o) * 2 + me_core},
                device_id_type=MESH,
            ).start()

    def send_other(d):
        wait_all(span_half.at[d, pl.ds(1, chips - 1)], half_rsem.at[d])
        pltpu.make_async_remote_copy(
            src_ref=span_half.at[d],
            dst_ref=span_other.at[d],
            send_sem=other_ssem.at[d],
            recv_sem=other_rsem.at[d],
            device_id={"trade": sibling},
            device_id_type=MESH,
        ).start()

    lag = max(1, (dates_own - 1) // 3)
    stages = ((max(1, lag // 2), send_cross), (2 * lag, send_half), (3 * lag, send_other))

    def exchange(turn):
        for late, done in stages:
            d = turn - late

            @pl.when(jnp.logical_and(d >= 0, d < dates_own))
            def _(d=d, done=done):
                done(d)

    @pl.loop(0, dates_own)
    def _(d):
        if n_path > 1:
            phase_one(d, path_local, path_total)
        send_pair(d)
        exchange(d)

    def grad_copy(g, o):
        return pltpu.make_async_remote_copy(
            src_ref=grad_send.at[g, o],
            dst_ref=grad_recv.at[me_trade],
            send_sem=grad_ssem.at[g, o],
            recv_sem=grad_rsem.at[me_trade],
            device_id={"path": path_at(-o), "trade": me_path * groups + g},
            device_id_type=MESH,
        )

    if n_path > 1:
        pl.semaphore_wait(ready_sem, n_path - 1)

    def gather_weights(d):
        wait_all(span_other.at[d], other_rsem.at[d])
        for o in range(chips):
            for core, source in ((me_core, span_half), (1 - me_core, span_other)):
                start = pl.multiple_of((chip_at(-o) * 2 + core) * rows, rows)
                slot_w[pl.ds(start, rows), :spans] = source[d, o]
        slot_w[:, spans:] = local_w[d]

    def sensitivities(d):
        for c in range(steps):
            cols = slice(c * chunk, (c + 1) * chunk)
            weight = dot(slot_w[...], table_t[:, cols]).astype(bf16)
            growth[d * steps + c] = weight * growth[d * steps + c]

    def factor_gradient(d):
        total = None
        for c in range(steps):
            sums = lax.dot_general(
                load_own[d, :, c * chunk : (c + 1) * chunk],
                growth[d * steps + c],
                (((1,), (1,)), ((), ())),
                preferred_element_type=f32,
            )
            total = sums if total is None else total + sums
        for o in range(n_path):
            grad_send[d // dates_out, o, lax.rem(d, dates_out)] = total[
                :, o * path_local : (o + 1) * path_local
            ]

    def send_gradient(d):
        g = d // dates_out

        @pl.when(lax.rem(d, dates_out) == dates_out - 1)
        def _():
            here = me_path * groups + g == me_trade

            @pl.when(here)
            def _():
                pltpu.make_async_copy(
                    grad_send.at[g, 0], grad_recv.at[me_trade], grad_rsem.at[me_trade]
                ).start()

            @pl.when(jnp.logical_not(here))
            def _():
                grad_copy(g, 0).start()

            for o in range(1, n_path):
                grad_copy(g, o).start()

    gather_weights(0)
    sensitivities(0)
    exchange(jnp.int32(dates_own))

    @pl.loop(1, dates_own)
    def _(d):
        gather_weights(d)
        factor_gradient(d - 1)
        sensitivities(d)
        exchange(dates_own + d)
        send_gradient(d - 1)

    factor_gradient(jnp.int32(dates_own - 1))
    send_gradient(jnp.int32(dates_own - 1))

    @pl.loop(0, dates_own // unroll)
    def _(block):
        for i in range(unroll):
            d = block * unroll + i
            for c in range(steps):
                loading_grad_ref[d, :, c * chunk : (c + 1) * chunk] = (
                    dot(fac[d], growth[d * steps + c]) / path_total
                )

    if n_path > 1:
        wait_all(fac_recv.at[pl.ds(1, n_path - 1)], fac_ssem)
    for d in range(dates_own):
        wait_all(pair_recv.at[d], pair_ssem.at[d])
        wait_all(cross_recv.at[d], cross_ssem.at[d])
        wait_all(span_half.at[d, pl.ds(1, chips - 1)], half_ssem.at[d])
        wait_all(span_other.at[d], other_ssem.at[d])
    for g in range(groups):

        @pl.when(me_path * groups + g != me_trade)
        def _():
            grad_copy(g, 0).wait_send()

        for o in range(1, n_path):
            grad_copy(g, o).wait_send()

    for b in range(n_trade):
        wait_all(grad_recv.at[b], grad_rsem.at[b])
    sums = grad_recv[0]
    for b in range(1, n_trade):
        sums = sums + grad_recv[b]
    factor_grad_ref[...] = sums


def on_device(
    n_path,
    n_trade,
    factors,
    loadings,
    notional,
    strike,
    date_weight,
    loss_spanning,
    loss_local,
    trade_slot,
    span_list,
):
    dates, factor_count, path_local = factors.shape
    trades = loadings.shape[2]
    spans = loss_spanning.shape[0]
    locals_ = loss_local.shape[0]
    span_slots = span_list.shape[0]
    width = spans + locals_
    paths = n_path * path_local
    rows = paths // n_trade
    chips = n_trade // 2
    dates_own = dates // n_path
    dates_out = dates // n_trade
    groups = dates_own // dates_out
    chunk = chunk_of(paths, trades)
    depth = 4 * factor_count
    results = 4 * factor_count * (dates_own * trades + dates_out * path_local)
    vmem = pl.BlockSpec(memory_space=pltpu.VMEM)
    dma = pltpu.SemaphoreType.DMA
    return pl.pallas_call(
        functools.partial(kernel, n_path, n_trade),
        out_shape=(
            pltpu.VMEM((dates_own, factor_count, trades), f32),
            pltpu.VMEM((dates_out, factor_count, path_local), f32),
        ),
        in_specs=[pl.BlockSpec(memory_space=pl.ANY)] * 9,
        out_specs=(vmem, vmem),
        scratch_shapes=[
            pltpu.VMEM((dates_own * (trades // chunk), paths, chunk), bf16),
            pltpu.VMEM((trades, width), bf16),
            pltpu.VMEM((width, trades), bf16),
            pltpu.VMEM((dates_own, factor_count, trades), bf16),
            pltpu.VMEM((dates_own, depth, trades), bf16),
            pltpu.VMEM((1, trades), f32),
            pltpu.VMEM((1, trades), f32),
            pltpu.VMEM((1, trades), f32),
            pltpu.SMEM((dates,), f32),
            pltpu.VMEM((1, spans), f32),
            pltpu.VMEM((1, locals_), f32),
            pltpu.VMEM((1, trades), jnp.int32),
            pltpu.VMEM((1, span_slots), jnp.int32),
            pltpu.VMEM((n_path, dates_own, factor_count, path_local), bf16),
            pltpu.VMEM((dates_own, factor_count, paths), bf16),
            pltpu.VMEM((dates_own, paths, depth), bf16),
            pltpu.VMEM((dates_own, 2, chips, rows, spans), f32),
            pltpu.VMEM((dates_own, chips, rows, spans), f32),
            pltpu.VMEM((dates_own, chips, rows, spans), f32),
            pltpu.VMEM((dates_own, chips - 1, rows, spans), f32),
            pltpu.VMEM((dates_own, paths, locals_), bf16),
            pltpu.VMEM((dates_own, chips, rows, spans), bf16),
            pltpu.VMEM((dates_own, chips, rows, spans), bf16),
            pltpu.VMEM((paths, width), bf16),
            pltpu.VMEM((groups, n_path, dates_out, factor_count, path_local), f32),
            pltpu.VMEM((n_trade, dates_out, factor_count, path_local), f32),
            pltpu.SemaphoreType.REGULAR,
            dma((9,)),
            dma,
            dma,
            dma((dates_own,)),
            dma((dates_own,)),
            dma((dates_own,)),
            dma((dates_own,)),
            dma((dates_own,)),
            dma((dates_own,)),
            dma((dates_own,)),
            dma((dates_own,)),
            dma((groups, n_path)),
            dma((n_trade,)),
        ],
        compiler_params=pltpu.CompilerParams(
            collective_id=0, has_side_effects=True, vmem_limit_bytes=vmem_bytes - results
        ),
    )(
        factors,
        loadings,
        notional[None],
        strike[None],
        date_weight,
        loss_spanning[None],
        loss_local[None],
        trade_slot[None],
        span_list[None],
    )


def solution(mesh):
    return jax.shard_map(
        functools.partial(on_device, mesh.shape["path"], mesh.shape["trade"]),
        mesh=mesh,
        in_specs=(
            P(None, None, "path"),
            P(None, None, "trade"),
            P("trade"),
            P("trade"),
            P(),
            P(),
            P("trade"),
            P("trade"),
            P("trade"),
        ),
        out_specs=(P("path", None, "trade"), P("trade", None, "path")),
        check_vma=False,
    )
```

```python
import functools
import math

import jax
import jax.numpy as jnp
from jax import lax
from jax.experimental import pallas as pl
from jax.experimental.pallas import tpu as pltpu
from jax.sharding import PartitionSpec as P

smoothing = 0.5
vmem_bytes = 254 << 18
MESH = pl.DeviceIdType.MESH
bf16 = jnp.bfloat16
f32 = jnp.float32


def chunk_of(paths, trades):
    return math.gcd(trades, (1 << 21) // paths)


def gathered_of(chunk):
    return (chunk // 4) // 128 * 128


def lane_gather(x, index):
    numbers = lax.GatherDimensionNumbers(
        offset_dims=(),
        collapsed_slice_dims=(1,),
        start_index_map=(1,),
        operand_batching_dims=(0,),
        start_indices_batching_dims=(0,),
    )
    return lax.gather(
        x,
        index[..., None],
        numbers,
        (1, 1),
        mode=lax.GatherScatterMode.PROMISE_IN_BOUNDS,
    )


def dot(a, b):
    return jnp.dot(a, b, preferred_element_type=f32)


def kernel(
    n_path,
    n_trade,
    factors_hbm,
    loadings_hbm,
    notional_hbm,
    strike_hbm,
    date_weight_hbm,
    loss_span_hbm,
    loss_local_hbm,
    slot_hbm,
    span_hbm,
    loading_grad_ref,
    factor_grad_ref,
    growth,
    table,
    table_t,
    place,
    load_own,
    load_split,
    notional_ref,
    strike_ref,
    offset,
    date_weight_ref,
    loss_span_ref,
    loss_local_ref,
    slot_ref,
    span_ref,
    fac_recv,
    fac,
    fac_split,
    part,
    pair_recv,
    chip_sum,
    cross_recv,
    local_w,
    span_half,
    span_other,
    slot_w,
    grad_send,
    grad_recv,
    ready_sem,
    in_sem,
    fac_ssem,
    fac_rsem,
    pair_ssem,
    pair_rsem,
    cross_ssem,
    cross_rsem,
    half_ssem,
    half_rsem,
    other_ssem,
    other_rsem,
    grad_ssem,
    grad_rsem,
):
    me_path = lax.axis_index("path")
    me_trade = lax.axis_index("trade")
    dates, factor_count, path_local = factors_hbm.shape
    dates_own = dates // n_path
    dates_out = dates // n_trade
    groups = dates_own // dates_out
    trades = loadings_hbm.shape[2]
    spans = loss_span_ref.shape[1]
    span_slots = span_ref.shape[1]
    locals_ = loss_local_ref.shape[1]
    slots = span_slots + locals_
    path_total = n_path * path_local
    chunk = chunk_of(path_total, trades)
    steps = trades // chunk
    first_date = me_path * dates_own
    rows = path_total // n_trade
    chips = n_trade // 2
    me_chip = me_trade // 2
    me_core = lax.rem(me_trade, 2)
    sibling = me_trade + 1 - 2 * me_core

    def path_at(step):
        return lax.rem(me_path + step + n_path, n_path)

    def trade_at(step):
        return lax.rem(me_trade + step + n_trade, n_trade)

    def chip_at(step):
        return lax.rem(me_chip + step + chips, chips)

    def columns(c):
        return pl.ds(pl.multiple_of(c * chunk, chunk), chunk)

    def wait_all(buffer, sem):
        pltpu.make_async_copy(buffer, buffer, sem).wait()

    barrier = pltpu.get_barrier_semaphore()
    for a in range(1, n_path):
        pl.semaphore_signal(
            barrier, inc=1, device_id={"path": path_at(a)}, device_id_type=MESH
        )
    for b in range(1, n_trade):
        pl.semaphore_signal(
            barrier, inc=1, device_id={"trade": trade_at(b)}, device_id_type=MESH
        )

    own_dates = pl.ds(first_date, dates_own)
    inputs = [
        pltpu.make_async_copy(source, target, in_sem.at[i])
        for i, (source, target) in enumerate(
            (
                (slot_hbm, slot_ref),
                (span_hbm, span_ref),
                (loadings_hbm.at[own_dates], load_own),
                (factors_hbm.at[own_dates], fac_recv.at[0]),
                (notional_hbm, notional_ref),
                (strike_hbm, strike_ref),
                (date_weight_hbm, date_weight_ref),
                (loss_span_hbm, loss_span_ref),
                (loss_local_hbm, loss_local_ref),
            )
        )
    ]
    for copy in inputs:
        copy.start()
    for copy in inputs[:2]:
        copy.wait()

    set_match = (
        lax.broadcasted_iota(jnp.int32, (spans, span_slots), 0) == span_ref[...]
    ).astype(f32).astype(bf16)

    @pl.loop(0, steps)
    def _(c):
        cols = columns(c)
        hot = (
            lax.broadcasted_iota(jnp.int32, (slots, chunk), 0) == slot_ref[:, cols]
        ).astype(f32)
        span_hot = dot(set_match, hot[:span_slots].astype(bf16))
        both = jnp.concatenate([span_hot, hot[span_slots:]], axis=0)
        table_t[:, cols] = both.astype(bf16)
        table[cols, :] = both.T.astype(bf16)

    for c in range(steps):
        for k in range((c + 1) * chunk - gathered_of(chunk), (c + 1) * chunk, 128):
            slot = jnp.broadcast_to(slot_ref[:, k : k + 128], (8, 128))
            column = slot - span_slots + spans
            for at in range(0, span_slots, 128):
                row = jnp.broadcast_to(span_ref[:, at : at + 128], (8, 128))
                span = lane_gather(row, jnp.bitwise_and(slot, 127))
                here = jnp.logical_and(slot >= at, slot < at + 128)
                column = jnp.where(here, span, column)
            place[0:1, k : k + 128] = jnp.bitwise_and(column, 127)[0:1]
            place[1:2, k : k + 128] = jnp.right_shift(column, 7)[0:1]

    for copy in inputs[2:]:
        copy.wait()

    pl.semaphore_wait(barrier, n_path + n_trade - 2)

    def fac_copy(o):
        there = path_at(o)
        return pltpu.make_async_remote_copy(
            src_ref=factors_hbm.at[pl.ds(there * dates_own, dates_own)],
            dst_ref=fac_recv.at[o],
            send_sem=fac_ssem,
            recv_sem=fac_rsem,
            device_id={"path": there},
            device_id_type=MESH,
        )

    for o in range(1, n_path):
        fac_copy(o).start()
    for o in range(1, n_path):
        pl.semaphore_signal(
            ready_sem, inc=1, device_id={"path": path_at(o)}, device_id_type=MESH
        )

    offset[...] = notional_ref[...] * strike_ref[...]

    @pl.loop(0, dates_own)
    def _(d):
        row = load_own[d]
        load_split[d] = jnp.concatenate([row, row, row, row], axis=0)

    def split_factors(first, last):
        @pl.loop(0, dates_own)
        def _(d):
            for o in range(first, last):
                block = fac_recv[o, d]
                at = pl.ds(o * path_local, path_local)
                fac[d, :, at] = block
                scaled = block.astype(f32) * f32(math.log2(math.e))
                high = scaled.astype(bf16).astype(f32)
                middle = (scaled - high).astype(bf16).astype(f32)
                low = scaled - high - middle
                split = [high, middle, low, jnp.zeros_like(low)]
                fac_split[d, at, :] = jnp.concatenate(split, axis=0).T.astype(bf16)

    def phase_one(d, first, last):
        at = slice(first, last)
        total = None
        for c in range(steps):
            cols = slice(c * chunk, (c + 1) * chunk)
            exponent = dot(fac_split[d, at, :], load_split[d, :, cols])
            grown = jnp.exp2(exponent) * notional_ref[:, cols]
            growth[d * steps + c, at, :] = grown.astype(bf16)
            values = (grown - offset[:, cols]).astype(bf16)
            sums = dot(values, table[cols, :])
            total = sums if total is None else total + sums

        for r in range(first // rows, last // rows):
            here = slice(r * rows - first, (r + 1) * rows - first)
            part[d, r % 2, r // 2] = total[here, :spans]
        weight = date_weight_ref[first_date + d]
        local_w[d, at, :] = (
            weight
            * loss_local_ref[...]
            * jax.nn.sigmoid(total[:, spans:] / smoothing)
        ).astype(bf16)

    split_factors(0, 1)
    unroll = math.gcd(dates_own, 4)

    @pl.loop(0, dates_own // unroll)
    def _(block):
        for i in range(unroll):
            phase_one(block * unroll + i, 0, path_local)

    if n_path > 1:
        wait_all(fac_recv.at[pl.ds(1, n_path - 1)], fac_rsem)
        split_factors(1, n_path)

    def send_pair(d):
        pltpu.make_async_remote_copy(
            src_ref=part.at[d, 1 - me_core],
            dst_ref=pair_recv.at[d],
            send_sem=pair_ssem.at[d],
            recv_sem=pair_rsem.at[d],
            device_id={"trade": sibling},
            device_id_type=MESH,
        ).start()

    def send_cross(d):
        wait_all(pair_recv.at[d], pair_rsem.at[d])
        chip_sum[d] = part[d, me_core] + pair_recv[d]
        for o in range(1, chips):
            there = chip_at(o)
            pltpu.make_async_remote_copy(
                src_ref=chip_sum.at[d, there],
                dst_ref=cross_recv.at[d, o - 1],
                send_sem=cross_ssem.at[d],
                recv_sem=cross_rsem.at[d],
                device_id={"trade": there * 2 + me_core},
                device_id_type=MESH,
            ).start()

    def send_half(d):
        wait_all(cross_recv.at[d], cross_rsem.at[d])
        sums = chip_sum[d, me_chip]
        for o in range(1, chips):
            sums = sums + cross_recv[d, o - 1]
        weight = date_weight_ref[first_date + d]
        span_half[d, 0] = (
            weight * loss_span_ref[...] * jax.nn.sigmoid(sums / smoothing)
        ).astype(bf16)
        for o in range(1, chips):
            pltpu.make_async_remote_copy(
                src_ref=span_half.at[d, 0],
                dst_ref=span_half.at[d, o],
                send_sem=half_ssem.at[d],
                recv_sem=half_rsem.at[d],
                device_id={"trade": chip_at(o) * 2 + me_core},
                device_id_type=MESH,
            ).start()

    def send_other(d):
        wait_all(span_half.at[d, pl.ds(1, chips - 1)], half_rsem.at[d])
        pltpu.make_async_remote_copy(
            src_ref=span_half.at[d],
            dst_ref=span_other.at[d],
            send_sem=other_ssem.at[d],
            recv_sem=other_rsem.at[d],
            device_id={"trade": sibling},
            device_id_type=MESH,
        ).start()

    lag = max(1, (dates_own - 1) // 3)
    stages = ((max(1, lag // 2), send_cross), (2 * lag, send_half), (3 * lag, send_other))

    def exchange(turn):
        for late, done in stages:
            d = turn - late

            @pl.when(jnp.logical_and(d >= 0, d < dates_own))
            def _(d=d, done=done):
                done(d)

    @pl.loop(0, dates_own)
    def _(d):
        if n_path > 1:
            phase_one(d, path_local, path_total)
        send_pair(d)
        exchange(d)

    def grad_copy(g, o):
        return pltpu.make_async_remote_copy(
            src_ref=grad_send.at[g, o],
            dst_ref=grad_recv.at[me_trade],
            send_sem=grad_ssem.at[g, o],
            recv_sem=grad_rsem.at[me_trade],
            device_id={"path": path_at(-o), "trade": me_path * groups + g},
            device_id_type=MESH,
        )

    if n_path > 1:
        pl.semaphore_wait(ready_sem, n_path - 1)

    def gather_weights(d):
        wait_all(span_other.at[d], other_rsem.at[d])
        for o in range(chips):
            for core, source in ((me_core, span_half), (1 - me_core, span_other)):
                start = pl.multiple_of((chip_at(-o) * 2 + core) * rows, rows)
                slot_w[pl.ds(start, rows), :spans] = source[d, o]
        slot_w[:, spans:] = local_w[d]

    def sensitivities(d):
        i16 = jnp.int16
        block = min(128, path_total)
        dense = chunk - gathered_of(chunk)
        for c in range(steps):
            now = growth.at[d * steps + c]
            for k in range(dense, chunk, 128):
                cols = slice(c * chunk + k, c * chunk + k + 128)
                lane = jnp.broadcast_to(place[0:1, cols], (block, 128)).astype(i16)
                group = jnp.broadcast_to(place[1:2, cols], (block, 128)).astype(i16)
                for r in range(0, path_total, block):
                    at = slice(r, r + block)
                    weight = lane_gather(slot_w[at, :128], lane)
                    for g in range(1, (spans + locals_) // 128):
                        other = lane_gather(slot_w[at, g * 128 : (g + 1) * 128], lane)
                        weight = jnp.where(group == g, other, weight)
                    now[at, k : k + 128] = weight * now[at, k : k + 128]
            cols = slice(c * chunk, c * chunk + dense)
            weight = dot(slot_w[...], table_t[:, cols]).astype(bf16)
            now[:, :dense] = weight * now[:, :dense]

    def factor_gradient(d):
        total = None
        for c in range(steps):
            sums = lax.dot_general(
                load_own[d, :, c * chunk : (c + 1) * chunk],
                growth[d * steps + c],
                (((1,), (1,)), ((), ())),
                preferred_element_type=f32,
            )
            total = sums if total is None else total + sums
        for o in range(n_path):
            grad_send[d // dates_out, o, lax.rem(d, dates_out)] = total[
                :, o * path_local : (o + 1) * path_local
            ]

    def send_gradient(d):
        g = d // dates_out

        @pl.when(lax.rem(d, dates_out) == dates_out - 1)
        def _():
            here = me_path * groups + g == me_trade

            @pl.when(here)
            def _():
                pltpu.make_async_copy(
                    grad_send.at[g, 0], grad_recv.at[me_trade], grad_rsem.at[me_trade]
                ).start()

            @pl.when(jnp.logical_not(here))
            def _():
                grad_copy(g, 0).start()

            for o in range(1, n_path):
                grad_copy(g, o).start()

    gather_weights(0)
    sensitivities(0)
    exchange(jnp.int32(dates_own))

    @pl.loop(1, dates_own)
    def _(d):
        gather_weights(d)
        factor_gradient(d - 1)
        sensitivities(d)
        exchange(dates_own + d)
        send_gradient(d - 1)

    factor_gradient(jnp.int32(dates_own - 1))
    send_gradient(jnp.int32(dates_own - 1))

    @pl.loop(0, dates_own // unroll)
    def _(block):
        for i in range(unroll):
            d = block * unroll + i
            for c in range(steps):
                loading_grad_ref[d, :, c * chunk : (c + 1) * chunk] = (
                    dot(fac[d], growth[d * steps + c]) / path_total
                )

    if n_path > 1:
        wait_all(fac_recv.at[pl.ds(1, n_path - 1)], fac_ssem)
    for d in range(dates_own):
        wait_all(pair_recv.at[d], pair_ssem.at[d])
        wait_all(cross_recv.at[d], cross_ssem.at[d])
        wait_all(span_half.at[d, pl.ds(1, chips - 1)], half_ssem.at[d])
        wait_all(span_other.at[d], other_ssem.at[d])
    for g in range(groups):

        @pl.when(me_path * groups + g != me_trade)
        def _():
            grad_copy(g, 0).wait_send()

        for o in range(1, n_path):
            grad_copy(g, o).wait_send()

    for b in range(n_trade):
        wait_all(grad_recv.at[b], grad_rsem.at[b])
    sums = grad_recv[0]
    for b in range(1, n_trade):
        sums = sums + grad_recv[b]
    factor_grad_ref[...] = sums


def on_device(
    n_path,
    n_trade,
    factors,
    loadings,
    notional,
    strike,
    date_weight,
    loss_spanning,
    loss_local,
    trade_slot,
    span_list,
):
    dates, factor_count, path_local = factors.shape
    trades = loadings.shape[2]
    spans = loss_spanning.shape[0]
    locals_ = loss_local.shape[0]
    span_slots = span_list.shape[0]
    width = spans + locals_
    paths = n_path * path_local
    rows = paths // n_trade
    chips = n_trade // 2
    dates_own = dates // n_path
    dates_out = dates // n_trade
    groups = dates_own // dates_out
    chunk = chunk_of(paths, trades)
    depth = 4 * factor_count
    results = 4 * factor_count * (dates_own * trades + dates_out * path_local)
    vmem = pl.BlockSpec(memory_space=pltpu.VMEM)
    dma = pltpu.SemaphoreType.DMA
    return pl.pallas_call(
        functools.partial(kernel, n_path, n_trade),
        out_shape=(
            pltpu.VMEM((dates_own, factor_count, trades), f32),
            pltpu.VMEM((dates_out, factor_count, path_local), f32),
        ),
        in_specs=[pl.BlockSpec(memory_space=pl.ANY)] * 9,
        out_specs=(vmem, vmem),
        scratch_shapes=[
            pltpu.VMEM((dates_own * (trades // chunk), paths, chunk), bf16),
            pltpu.VMEM((trades, width), bf16),
            pltpu.VMEM((width, trades), bf16),
            pltpu.VMEM((2, trades), jnp.int32),
            pltpu.VMEM((dates_own, factor_count, trades), bf16),
            pltpu.VMEM((dates_own, depth, trades), bf16),
            pltpu.VMEM((1, trades), f32),
            pltpu.VMEM((1, trades), f32),
            pltpu.VMEM((1, trades), f32),
            pltpu.SMEM((dates,), f32),
            pltpu.VMEM((1, spans), f32),
            pltpu.VMEM((1, locals_), f32),
            pltpu.VMEM((1, trades), jnp.int32),
            pltpu.VMEM((1, span_slots), jnp.int32),
            pltpu.VMEM((n_path, dates_own, factor_count, path_local), bf16),
            pltpu.VMEM((dates_own, factor_count, paths), bf16),
            pltpu.VMEM((dates_own, paths, depth), bf16),
            pltpu.VMEM((dates_own, 2, chips, rows, spans), f32),
            pltpu.VMEM((dates_own, chips, rows, spans), f32),
            pltpu.VMEM((dates_own, chips, rows, spans), f32),
            pltpu.VMEM((dates_own, chips - 1, rows, spans), f32),
            pltpu.VMEM((dates_own, paths, locals_), bf16),
            pltpu.VMEM((dates_own, chips, rows, spans), bf16),
            pltpu.VMEM((dates_own, chips, rows, spans), bf16),
            pltpu.VMEM((paths, width), bf16),
            pltpu.VMEM((groups, n_path, dates_out, factor_count, path_local), f32),
            pltpu.VMEM((n_trade, dates_out, factor_count, path_local), f32),
            pltpu.SemaphoreType.REGULAR,
            dma((9,)),
            dma,
            dma,
            dma((dates_own,)),
            dma((dates_own,)),
            dma((dates_own,)),
            dma((dates_own,)),
            dma((dates_own,)),
            dma((dates_own,)),
            dma((dates_own,)),
            dma((dates_own,)),
            dma((groups, n_path)),
            dma((n_trade,)),
        ],
        compiler_params=pltpu.CompilerParams(
            collective_id=0, has_side_effects=True, vmem_limit_bytes=vmem_bytes - results
        ),
    )(
        factors,
        loadings,
        notional[None],
        strike[None],
        date_weight,
        loss_spanning[None],
        loss_local[None],
        trade_slot[None],
        span_list[None],
    )


def solution(mesh):
    return jax.shard_map(
        functools.partial(on_device, mesh.shape["path"], mesh.shape["trade"]),
        mesh=mesh,
        in_specs=(
            P(None, None, "path"),
            P(None, None, "trade"),
            P("trade"),
            P("trade"),
            P(),
            P(),
            P("trade"),
            P("trade"),
            P("trade"),
        ),
        out_specs=(P("path", None, "trade"), P("trade", None, "path")),
        check_vma=False,
    )
```

```python
import functools
import math

import jax
import jax.numpy as jnp
from jax import lax
from jax.experimental import pallas as pl
from jax.experimental.pallas import tpu as pltpu
from jax.sharding import PartitionSpec as P

smoothing = 0.5
vmem_bytes = 254 << 18
MESH = pl.DeviceIdType.MESH
bf16 = jnp.bfloat16
f32 = jnp.float32


def chunk_of(paths, trades):
    return math.gcd(trades, (1 << 21) // paths)


def gathered_of(chunk):
    return (3 * chunk // 8) // 128 * 128


def lane_gather(x, index):
    numbers = lax.GatherDimensionNumbers(
        offset_dims=(),
        collapsed_slice_dims=(1,),
        start_index_map=(1,),
        operand_batching_dims=(0,),
        start_indices_batching_dims=(0,),
    )
    return lax.gather(
        x,
        index[..., None],
        numbers,
        (1, 1),
        mode=lax.GatherScatterMode.PROMISE_IN_BOUNDS,
    )


def dot(a, b):
    return jnp.dot(a, b, preferred_element_type=f32)


def kernel(
    n_path,
    n_trade,
    factors_hbm,
    loadings_hbm,
    notional_hbm,
    strike_hbm,
    date_weight_hbm,
    loss_span_hbm,
    loss_local_hbm,
    slot_hbm,
    span_hbm,
    loading_grad_ref,
    factor_grad_ref,
    growth,
    table,
    table_t,
    place,
    load_own,
    load_split,
    notional_ref,
    strike_ref,
    offset,
    date_weight_ref,
    loss_span_ref,
    loss_local_ref,
    slot_ref,
    span_ref,
    fac_recv,
    fac,
    fac_split,
    part,
    pair_recv,
    chip_sum,
    cross_recv,
    local_w,
    span_half,
    span_other,
    slot_w,
    grad_send,
    grad_recv,
    ready_sem,
    in_sem,
    fac_ssem,
    fac_rsem,
    pair_ssem,
    pair_rsem,
    cross_ssem,
    cross_rsem,
    half_ssem,
    half_rsem,
    other_ssem,
    other_rsem,
    grad_ssem,
    grad_rsem,
):
    me_path = lax.axis_index("path")
    me_trade = lax.axis_index("trade")
    dates, factor_count, path_local = factors_hbm.shape
    dates_own = dates // n_path
    dates_out = dates // n_trade
    groups = dates_own // dates_out
    trades = loadings_hbm.shape[2]
    spans = loss_span_ref.shape[1]
    span_slots = span_ref.shape[1]
    locals_ = loss_local_ref.shape[1]
    slots = span_slots + locals_
    path_total = n_path * path_local
    chunk = chunk_of(path_total, trades)
    steps = trades // chunk
    first_date = me_path * dates_own
    rows = path_total // n_trade
    chips = n_trade // 2
    me_chip = me_trade // 2
    me_core = lax.rem(me_trade, 2)
    sibling = me_trade + 1 - 2 * me_core

    def path_at(step):
        return lax.rem(me_path + step + n_path, n_path)

    def trade_at(step):
        return lax.rem(me_trade + step + n_trade, n_trade)

    def chip_at(step):
        return lax.rem(me_chip + step + chips, chips)

    def columns(c):
        return pl.ds(pl.multiple_of(c * chunk, chunk), chunk)

    def wait_all(buffer, sem):
        pltpu.make_async_copy(buffer, buffer, sem).wait()

    barrier = pltpu.get_barrier_semaphore()
    for a in range(1, n_path):
        pl.semaphore_signal(
            barrier, inc=1, device_id={"path": path_at(a)}, device_id_type=MESH
        )
    for b in range(1, n_trade):
        pl.semaphore_signal(
            barrier, inc=1, device_id={"trade": trade_at(b)}, device_id_type=MESH
        )

    own_dates = pl.ds(first_date, dates_own)
    inputs = [
        pltpu.make_async_copy(source, target, in_sem.at[i])
        for i, (source, target) in enumerate(
            (
                (slot_hbm, slot_ref),
                (span_hbm, span_ref),
                (loadings_hbm.at[own_dates], load_own),
                (factors_hbm.at[own_dates], fac_recv.at[0]),
                (notional_hbm, notional_ref),
                (strike_hbm, strike_ref),
                (date_weight_hbm, date_weight_ref),
                (loss_span_hbm, loss_span_ref),
                (loss_local_hbm, loss_local_ref),
            )
        )
    ]
    for copy in inputs:
        copy.start()
    for copy in inputs[:2]:
        copy.wait()

    set_match = (
        lax.broadcasted_iota(jnp.int32, (spans, span_slots), 0) == span_ref[...]
    ).astype(f32).astype(bf16)

    @pl.loop(0, steps)
    def _(c):
        cols = columns(c)
        hot = (
            lax.broadcasted_iota(jnp.int32, (slots, chunk), 0) == slot_ref[:, cols]
        ).astype(f32)
        span_hot = dot(set_match, hot[:span_slots].astype(bf16))
        both = jnp.concatenate([span_hot, hot[span_slots:]], axis=0)
        table_t[:, cols] = both.astype(bf16)
        table[cols, :] = both.T.astype(bf16)

    for c in range(steps):
        for k in range((c + 1) * chunk - gathered_of(chunk), (c + 1) * chunk, 128):
            slot = jnp.broadcast_to(slot_ref[:, k : k + 128], (8, 128))
            column = slot - span_slots + spans
            for at in range(0, span_slots, 128):
                row = jnp.broadcast_to(span_ref[:, at : at + 128], (8, 128))
                span = lane_gather(row, jnp.bitwise_and(slot, 127))
                here = jnp.logical_and(slot >= at, slot < at + 128)
                column = jnp.where(here, span, column)
            place[0:1, k : k + 128] = jnp.bitwise_and(column, 127)[0:1]
            place[1:2, k : k + 128] = jnp.right_shift(column, 7)[0:1]

    for copy in inputs[2:]:
        copy.wait()

    pl.semaphore_wait(barrier, n_path + n_trade - 2)

    def fac_copy(o):
        there = path_at(o)
        return pltpu.make_async_remote_copy(
            src_ref=factors_hbm.at[pl.ds(there * dates_own, dates_own)],
            dst_ref=fac_recv.at[o],
            send_sem=fac_ssem,
            recv_sem=fac_rsem,
            device_id={"path": there},
            device_id_type=MESH,
        )

    for o in range(1, n_path):
        fac_copy(o).start()
    for o in range(1, n_path):
        pl.semaphore_signal(
            ready_sem, inc=1, device_id={"path": path_at(o)}, device_id_type=MESH
        )

    offset[...] = notional_ref[...] * strike_ref[...]

    @pl.loop(0, dates_own)
    def _(d):
        row = load_own[d]
        load_split[d] = jnp.concatenate([row, row, row, row], axis=0)

    def split_factors(first, last):
        @pl.loop(0, dates_own)
        def _(d):
            for o in range(first, last):
                block = fac_recv[o, d]
                at = pl.ds(o * path_local, path_local)
                fac[d, :, at] = block
                scaled = block.astype(f32) * f32(math.log2(math.e))
                high = scaled.astype(bf16).astype(f32)
                middle = (scaled - high).astype(bf16).astype(f32)
                low = scaled - high - middle
                split = [high, middle, low, jnp.zeros_like(low)]
                fac_split[d, at, :] = jnp.concatenate(split, axis=0).T.astype(bf16)

    def phase_one(d, first, last):
        at = slice(first, last)
        total = None
        for c in range(steps):
            cols = slice(c * chunk, (c + 1) * chunk)
            exponent = dot(fac_split[d, at, :], load_split[d, :, cols])
            grown = jnp.exp2(exponent) * notional_ref[:, cols]
            growth[d * steps + c, at, :] = grown.astype(bf16)
            values = (grown - offset[:, cols]).astype(bf16)
            sums = dot(values, table[cols, :])
            total = sums if total is None else total + sums

        for r in range(first // rows, last // rows):
            here = slice(r * rows - first, (r + 1) * rows - first)
            part[d, r % 2, r // 2] = total[here, :spans]
        weight = date_weight_ref[first_date + d]
        local_w[d, at, :] = (
            weight
            * loss_local_ref[...]
            * jax.nn.sigmoid(total[:, spans:] / smoothing)
        ).astype(bf16)

    split_factors(0, 1)
    unroll = math.gcd(dates_own, 4)

    @pl.loop(0, dates_own // unroll)
    def _(block):
        for i in range(unroll):
            phase_one(block * unroll + i, 0, path_local)

    if n_path > 1:
        wait_all(fac_recv.at[pl.ds(1, n_path - 1)], fac_rsem)
        split_factors(1, n_path)

    def send_pair(d):
        pltpu.make_async_remote_copy(
            src_ref=part.at[d, 1 - me_core],
            dst_ref=pair_recv.at[d],
            send_sem=pair_ssem.at[d],
            recv_sem=pair_rsem.at[d],
            device_id={"trade": sibling},
            device_id_type=MESH,
        ).start()

    def send_cross(d):
        wait_all(pair_recv.at[d], pair_rsem.at[d])
        chip_sum[d] = part[d, me_core] + pair_recv[d]
        for o in range(1, chips):
            there = chip_at(o)
            pltpu.make_async_remote_copy(
                src_ref=chip_sum.at[d, there],
                dst_ref=cross_recv.at[d, o - 1],
                send_sem=cross_ssem.at[d],
                recv_sem=cross_rsem.at[d],
                device_id={"trade": there * 2 + me_core},
                device_id_type=MESH,
            ).start()

    def send_half(d):
        wait_all(cross_recv.at[d], cross_rsem.at[d])
        sums = chip_sum[d, me_chip]
        for o in range(1, chips):
            sums = sums + cross_recv[d, o - 1]
        weight = date_weight_ref[first_date + d]
        span_half[d, 0] = (
            weight * loss_span_ref[...] * jax.nn.sigmoid(sums / smoothing)
        ).astype(bf16)
        for o in range(1, chips):
            pltpu.make_async_remote_copy(
                src_ref=span_half.at[d, 0],
                dst_ref=span_half.at[d, o],
                send_sem=half_ssem.at[d],
                recv_sem=half_rsem.at[d],
                device_id={"trade": chip_at(o) * 2 + me_core},
                device_id_type=MESH,
            ).start()

    def send_other(d):
        wait_all(span_half.at[d, pl.ds(1, chips - 1)], half_rsem.at[d])
        pltpu.make_async_remote_copy(
            src_ref=span_half.at[d],
            dst_ref=span_other.at[d],
            send_sem=other_ssem.at[d],
            recv_sem=other_rsem.at[d],
            device_id={"trade": sibling},
            device_id_type=MESH,
        ).start()

    lag = max(1, (dates_own - 1) // 3)
    stages = ((max(1, lag // 2), send_cross), (2 * lag, send_half), (3 * lag, send_other))

    def exchange(turn):
        for late, done in stages:
            d = turn - late

            @pl.when(jnp.logical_and(d >= 0, d < dates_own))
            def _(d=d, done=done):
                done(d)

    @pl.loop(0, dates_own)
    def _(d):
        if n_path > 1:
            phase_one(d, path_local, path_total)
        send_pair(d)
        exchange(d)

    def grad_copy(g, o):
        return pltpu.make_async_remote_copy(
            src_ref=grad_send.at[g, o],
            dst_ref=grad_recv.at[me_trade],
            send_sem=grad_ssem.at[g, o],
            recv_sem=grad_rsem.at[me_trade],
            device_id={"path": path_at(-o), "trade": me_path * groups + g},
            device_id_type=MESH,
        )

    if n_path > 1:
        pl.semaphore_wait(ready_sem, n_path - 1)

    def gather_weights(d):
        wait_all(span_other.at[d], other_rsem.at[d])
        for o in range(chips):
            for core, source in ((me_core, span_half), (1 - me_core, span_other)):
                start = pl.multiple_of((chip_at(-o) * 2 + core) * rows, rows)
                slot_w[pl.ds(start, rows), :spans] = source[d, o]
        slot_w[:, spans:] = local_w[d]

    def sensitivities(d):
        i16 = jnp.int16
        block = min(128, path_total)
        dense = chunk - gathered_of(chunk)
        for c in range(steps):
            now = growth.at[d * steps + c]
            for k in range(dense, chunk, 128):
                cols = slice(c * chunk + k, c * chunk + k + 128)
                lane = jnp.broadcast_to(place[0:1, cols], (block, 128)).astype(i16)
                group = jnp.broadcast_to(place[1:2, cols], (block, 128)).astype(i16)
                for r in range(0, path_total, block):
                    at = slice(r, r + block)
                    weight = lane_gather(slot_w[at, :128], lane)
                    for g in range(1, (spans + locals_) // 128):
                        other = lane_gather(slot_w[at, g * 128 : (g + 1) * 128], lane)
                        weight = jnp.where(group == g, other, weight)
                    now[at, k : k + 128] = weight * now[at, k : k + 128]
            cols = slice(c * chunk, c * chunk + dense)
            weight = dot(slot_w[...], table_t[:, cols]).astype(bf16)
            now[:, :dense] = weight * now[:, :dense]

    def factor_gradient(d):
        total = None
        for c in range(steps):
            sums = lax.dot_general(
                load_own[d, :, c * chunk : (c + 1) * chunk],
                growth[d * steps + c],
                (((1,), (1,)), ((), ())),
                preferred_element_type=f32,
            )
            total = sums if total is None else total + sums
        for o in range(n_path):
            grad_send[d // dates_out, o, lax.rem(d, dates_out)] = total[
                :, o * path_local : (o + 1) * path_local
            ]

    def send_gradient(d):
        g = d // dates_out

        @pl.when(lax.rem(d, dates_out) == dates_out - 1)
        def _():
            here = me_path * groups + g == me_trade

            @pl.when(here)
            def _():
                pltpu.make_async_copy(
                    grad_send.at[g, 0], grad_recv.at[me_trade], grad_rsem.at[me_trade]
                ).start()

            @pl.when(jnp.logical_not(here))
            def _():
                grad_copy(g, 0).start()

            for o in range(1, n_path):
                grad_copy(g, o).start()

    gather_weights(0)
    sensitivities(0)
    exchange(jnp.int32(dates_own))

    @pl.loop(1, dates_own)
    def _(d):
        gather_weights(d)
        factor_gradient(d - 1)
        sensitivities(d)
        exchange(dates_own + d)
        send_gradient(d - 1)

    factor_gradient(jnp.int32(dates_own - 1))
    send_gradient(jnp.int32(dates_own - 1))

    @pl.loop(0, dates_own // unroll)
    def _(block):
        for i in range(unroll):
            d = block * unroll + i
            for c in range(steps):
                loading_grad_ref[d, :, c * chunk : (c + 1) * chunk] = (
                    dot(fac[d], growth[d * steps + c]) / path_total
                )

    if n_path > 1:
        wait_all(fac_recv.at[pl.ds(1, n_path - 1)], fac_ssem)
    for d in range(dates_own):
        wait_all(pair_recv.at[d], pair_ssem.at[d])
        wait_all(cross_recv.at[d], cross_ssem.at[d])
        wait_all(span_half.at[d, pl.ds(1, chips - 1)], half_ssem.at[d])
        wait_all(span_other.at[d], other_ssem.at[d])
    for g in range(groups):

        @pl.when(me_path * groups + g != me_trade)
        def _():
            grad_copy(g, 0).wait_send()

        for o in range(1, n_path):
            grad_copy(g, o).wait_send()

    for b in range(n_trade):
        wait_all(grad_recv.at[b], grad_rsem.at[b])
    sums = grad_recv[0]
    for b in range(1, n_trade):
        sums = sums + grad_recv[b]
    factor_grad_ref[...] = sums


def on_device(
    n_path,
    n_trade,
    factors,
    loadings,
    notional,
    strike,
    date_weight,
    loss_spanning,
    loss_local,
    trade_slot,
    span_list,
):
    dates, factor_count, path_local = factors.shape
    trades = loadings.shape[2]
    spans = loss_spanning.shape[0]
    locals_ = loss_local.shape[0]
    span_slots = span_list.shape[0]
    width = spans + locals_
    paths = n_path * path_local
    rows = paths // n_trade
    chips = n_trade // 2
    dates_own = dates // n_path
    dates_out = dates // n_trade
    groups = dates_own // dates_out
    chunk = chunk_of(paths, trades)
    depth = 4 * factor_count
    results = 4 * factor_count * (dates_own * trades + dates_out * path_local)
    vmem = pl.BlockSpec(memory_space=pltpu.VMEM)
    dma = pltpu.SemaphoreType.DMA
    return pl.pallas_call(
        functools.partial(kernel, n_path, n_trade),
        out_shape=(
            pltpu.VMEM((dates_own, factor_count, trades), f32),
            pltpu.VMEM((dates_out, factor_count, path_local), f32),
        ),
        in_specs=[pl.BlockSpec(memory_space=pl.ANY)] * 9,
        out_specs=(vmem, vmem),
        scratch_shapes=[
            pltpu.VMEM((dates_own * (trades // chunk), paths, chunk), bf16),
            pltpu.VMEM((trades, width), bf16),
            pltpu.VMEM((width, trades), bf16),
            pltpu.VMEM((2, trades), jnp.int32),
            pltpu.VMEM((dates_own, factor_count, trades), bf16),
            pltpu.VMEM((dates_own, depth, trades), bf16),
            pltpu.VMEM((1, trades), f32),
            pltpu.VMEM((1, trades), f32),
            pltpu.VMEM((1, trades), f32),
            pltpu.SMEM((dates,), f32),
            pltpu.VMEM((1, spans), f32),
            pltpu.VMEM((1, locals_), f32),
            pltpu.VMEM((1, trades), jnp.int32),
            pltpu.VMEM((1, span_slots), jnp.int32),
            pltpu.VMEM((n_path, dates_own, factor_count, path_local), bf16),
            pltpu.VMEM((dates_own, factor_count, paths), bf16),
            pltpu.VMEM((dates_own, paths, depth), bf16),
            pltpu.VMEM((dates_own, 2, chips, rows, spans), f32),
            pltpu.VMEM((dates_own, chips, rows, spans), f32),
            pltpu.VMEM((dates_own, chips, rows, spans), f32),
            pltpu.VMEM((dates_own, chips - 1, rows, spans), f32),
            pltpu.VMEM((dates_own, paths, locals_), bf16),
            pltpu.VMEM((dates_own, chips, rows, spans), bf16),
            pltpu.VMEM((dates_own, chips, rows, spans), bf16),
            pltpu.VMEM((paths, width), bf16),
            pltpu.VMEM((groups, n_path, dates_out, factor_count, path_local), f32),
            pltpu.VMEM((n_trade, dates_out, factor_count, path_local), f32),
            pltpu.SemaphoreType.REGULAR,
            dma((9,)),
            dma,
            dma,
            dma((dates_own,)),
            dma((dates_own,)),
            dma((dates_own,)),
            dma((dates_own,)),
            dma((dates_own,)),
            dma((dates_own,)),
            dma((dates_own,)),
            dma((dates_own,)),
            dma((groups, n_path)),
            dma((n_trade,)),
        ],
        compiler_params=pltpu.CompilerParams(
            collective_id=0, has_side_effects=True, vmem_limit_bytes=vmem_bytes - results
        ),
    )(
        factors,
        loadings,
        notional[None],
        strike[None],
        date_weight,
        loss_spanning[None],
        loss_local[None],
        trade_slot[None],
        span_list[None],
    )


def solution(mesh):
    return jax.shard_map(
        functools.partial(on_device, mesh.shape["path"], mesh.shape["trade"]),
        mesh=mesh,
        in_specs=(
            P(None, None, "path"),
            P(None, None, "trade"),
            P("trade"),
            P("trade"),
            P(),
            P(),
            P("trade"),
            P("trade"),
            P("trade"),
        ),
        out_specs=(P("path", None, "trade"), P("trade", None, "path")),
        check_vma=False,
    )
```
